512 devices in a mesh: dp: 64 (over x, z), mp: 8 (over y, core).
Axes of the slice: x: 4, y: 4, z: 16, core: 2. Of those that a mesh axis runs over, the one named last changes fastest.
Arguments:
- layer_input: float32 [16384, 512], P('dp'), may hold values from -6 to 6
- grad_out: float32 [16384, 512], P('dp'), may hold values from -6 to 6
- segment: int32 [64, 256], P('dp'), may hold values from 0 to 7, never falling along the last dimension, each value on 1 to 128 neighbouring positions
- item_ids: int32 [16384], P('dp'), may hold values from 0 to 511
- w_uvqk: float32 [512, 2048], P(None, 'mp'), may hold values from -0.25 to 0.25
- w_out: float32 [512, 512], P('mp'), may hold values from -0.25 to 0.25
- table: float32 [512, 512], P(('dp', 'mp')), may hold values from -6 to 6
- accum: float32 [512], P(('dp', 'mp')), may hold values from 0.1 to 2
Outputs:
- w_uvqk_grad: float32 [512, 2048], P(None, 'mp')
- w_out_grad: float32 [512, 512], P('mp')
- new_table: float32 [512, 512], P(('dp', 'mp'))
- new_accum: float32 [512], P(('dp', 'mp'))
The draws below stay inside these ranges and needn't reach their ends.
Inputs may be any that keep to these rules, and one draw needn't show every extreme that they name: `segment`: segment numbers never fall along a row; a history holds at most 128 tokens and some history holds exactly that many.
All inputs are finite; a program needn't handle non-finite values.
Results may differ from the reference program's by a relative error of at most 0.0003.
Values sent between devices are 32-bit elements; how exact they have to be, the bound alone decides.
No kernel may reach another device: no remote copies, remote signals or barrier semaphores. Data moves between devices by JAX's collectives and lax.ppermute only.
A program may use at most 64 MiB of HBM per device.

```python
import math
import jax
import jax.numpy as jnp
import numpy as np
from jax import lax

D = 512
HEADS = 8
HEAD_DIM = 64
TOK_DEV = 256
SEQ_DEV = 8
SEQ_MOST = 128
TOKENS = 16384
ROWS = 512
N_DP = 64


def plant(array, own_key, low, high):
    spot = [jax.random.randint(jax.random.fold_in(own_key, axis), (), 0, length) for axis, length in enumerate(array.shape)]
    main_axis = array.shape.index(max(array.shape))
    next_to = spot[:main_axis] + [(spot[main_axis] + 1) % array.shape[main_axis]] + spot[main_axis + 1:]
    return array.at[tuple(spot)].set(low).at[tuple(next_to)].set(high)


def steps_of(stream_key, dims, cuts, low, high):
    def one(dim, parts):
        draws = jax.random.uniform(jax.random.fold_in(jax.random.fold_in(stream_key, 6), dim), (parts,), jnp.float32, low / len(cuts), high / len(cuts))
        return jnp.repeat(jnp.exp(draws), dims[dim] // parts).reshape((-1,) + (1,) * (len(dims) - dim - 1))

    factor_of = one(*cuts[0])
    for cut in cuts[1:]:
        factor_of = factor_of * one(*cut)
    return factor_of


def rank_table(number_of, skew):
    weights = [(1 << 20) // math.isqrt(standing ** skew) + 1 for standing in range(1, number_of + 1)]
    spread = 1 + sum(weights) // (1 << 30)
    return np.cumsum(np.array([max(1, weight // spread) for weight in weights]))


def ranked_ids(own_key, extent, number_of, skew):
    grid = rank_table(number_of, skew)
    ticket = jax.random.randint(jax.random.fold_in(own_key, 1), extent, 0, int(grid[number_of - 1]))
    grade = jnp.searchsorted(jnp.asarray(grid, jnp.int32), ticket, side="right")
    return jax.random.permutation(jax.random.fold_in(own_key, 2), number_of)[grade].astype(jnp.int32)


def profile(amount, total, reach, skew):
    loads = [(1 << 20) // math.isqrt(standing ** skew) + 1 for standing in range(2, amount + 1)]
    surplus, given = total - reach - (amount - 1), [1] * (amount - 1)
    while surplus > 0:
        candidates = [i for i in range(amount - 1) if given[i] < reach]
        pool, remaining = sum([loads[i] for i in candidates]), surplus
        for i in candidates:
            more = min(reach - given[i], max(1, remaining * loads[i] // pool), surplus)
            given[i] = given[i] + more
            surplus = surplus - more
    return np.array([reach] + given)


def uneven(key, number_of, total, limit, lean):
    if number_of == 2:
        one = jax.random.randint(key, (), max(1, total - limit), min(limit, total - 1) + 1)
        return jnp.stack([one, total - one])
    tallies = jnp.asarray(profile(number_of, total, limit, lean), jnp.int32)
    pairs = (number_of - 1) // 2
    giver, sink = tallies[1:1 + 2 * pairs:2], tallies[2:2 + 2 * pairs:2]
    margin = jnp.minimum(giver - 1, limit - sink)
    moved = jax.random.randint(jax.random.fold_in(key, 1), (pairs,), 0, 1 << 20) % (margin + 1)
    tallies = tallies.at[1:1 + 2 * pairs:2].set(giver - moved).at[2:2 + 2 * pairs:2].set(sink + moved)
    return tallies[jax.random.permutation(jax.random.fold_in(key, 2), number_of)]


def normal_values(stream_key, extent, spread, most, cuts=(), dtype=jnp.bfloat16):
    entries = spread * jax.random.normal(stream_key, extent, jnp.float32)
    if cuts:
        entries = entries * steps_of(stream_key, extent, cuts, -0.22, 0.18)
    return jnp.clip(entries, -most, most).astype(dtype)


def setup_inputs(seed: int = 0) -> dict:
    seeds = jax.random.split(jax.random.key(seed), 9)
    return {
        "layer_input": normal_values(seeds[0], (TOKENS, D), 1.0, 6.0, ((0, 64),), jnp.float32),
        "grad_out": normal_values(seeds[1], (TOKENS, D), 1.0, 6.0, ((0, 64),), jnp.float32),
        "segment": jax.vmap(lambda own: jnp.searchsorted(jnp.cumsum(uneven(own, SEQ_DEV, TOK_DEV, SEQ_MOST, 2)), jnp.arange(TOK_DEV), side="right"))(jax.random.split(seeds[2], N_DP)).reshape((N_DP, TOK_DEV)).astype(jnp.int32),
        "item_ids": plant(ranked_ids(seeds[3], (TOKENS,), ROWS, 2), jax.random.fold_in(seeds[3], 3), 0, ROWS - 1).astype(jnp.int32),
        "w_uvqk": normal_values(seeds[4], (D, 4 * D), D ** -0.5, 0.25, ((1, 8),), jnp.float32),
        "w_out": normal_values(seeds[5], (D, D), D ** -0.5, 0.25, ((0, 8),), jnp.float32),
        "table": normal_values(seeds[6], (ROWS, D), 1.0, 6.0, ((0, 512),), jnp.float32),
        "accum": jnp.clip(jnp.exp(math.log(2.0) - 2.9957323 * jax.random.uniform(seeds[7], (ROWS,), jnp.float32) ** steps_of(seeds[7], (ROWS,), ((0, 512),), -0.2, 0.2)), 0.1, 2.0),
    }


highest = lax.Precision.HIGHEST

def mdot(left, right):
    return jnp.dot(left, right, precision=highest, preferred_element_type=jnp.float32)

def group_grads(layer_input, grad_out, segment, w_uvqk, w_out):
    count = layer_input.shape[0]
    scale = HEAD_DIM ** (-0.5)
    pre = mdot(layer_input, w_uvqk).reshape(count, HEADS, 4, HEAD_DIM)
    act = jax.nn.silu(pre)
    ublk, vblk, qblk, kblk = (act[:, :, 0], act[:, :, 1], act[:, :, 2], act[:, :, 3])
    place = jnp.arange(count)
    mask = ((segment[:, None] == segment[None, :]) & (place[:, None] >= place[None, :])).astype(jnp.float32)
    score = jnp.einsum('ihd,jhd->hij', qblk, kblk, precision=highest) * scale
    sigm = jax.nn.sigmoid(score)
    attn = score * sigm * mask
    outv = jnp.einsum('hij,jhd->ihd', attn, vblk, precision=highest).reshape(count, D)
    mean = lax.optimization_barrier(jnp.sum(outv, axis=1, keepdims=True)) / D
    var = lax.optimization_barrier(jnp.sum(outv * outv, axis=1, keepdims=True)) / D - mean * mean
    rstd = lax.rsqrt(var + 1e-05)
    normed = (outv - mean) * rstd
    nheads = normed.reshape(count, HEADS, HEAD_DIM)
    zval = (nheads * ublk).reshape(count, D)
    dzval = mdot(grad_out, w_out.T).reshape(count, HEADS, HEAD_DIM)
    w_out_grad = mdot(zval.T, grad_out)
    dnorm = (dzval * ublk).reshape(count, D)
    dublk = dzval * nheads
    first = lax.optimization_barrier(jnp.sum(dnorm, axis=1, keepdims=True)) / D
    second = lax.optimization_barrier(jnp.sum(dnorm * normed, axis=1, keepdims=True)) / D
    dout = (rstd * (dnorm - first - normed * second)).reshape(count, HEADS, HEAD_DIM)
    dattn = jnp.einsum('ihd,jhd->hij', dout, vblk, precision=highest)
    dvblk = jnp.einsum('hij,ihd->jhd', attn, dout, precision=highest)
    dscore = dattn * mask * (sigm * (1.0 + score * (1.0 - sigm))) * scale
    dqblk = jnp.einsum('hij,jhd->ihd', dscore, kblk, precision=highest)
    dkblk = jnp.einsum('hij,ihd->jhd', dscore, qblk, precision=highest)
    dact = jnp.stack([dublk, dvblk, dqblk, dkblk], axis=2)
    psig = jax.nn.sigmoid(pre)
    dpre = (dact * psig * (1.0 + pre * (1.0 - psig))).reshape(count, 4 * D)
    w_uvqk_grad = mdot(layer_input.T, dpre)
    x_grad = grad_out + mdot(dpre, w_uvqk.T)
    return (w_uvqk_grad, w_out_grad, x_grad)

def reference(layer_input, grad_out, segment, item_ids, w_uvqk, w_out, table, accum):
    groups = segment.shape[0]
    inputs = layer_input.reshape(groups, TOK_DEV, D)
    cotans = grad_out.reshape(groups, TOK_DEV, D)

    def step(carry, pieces):
        one, two, three = group_grads(pieces[0], pieces[1], pieces[2], w_uvqk, w_out)
        return ((carry[0] + one, carry[1] + two), three)
    start = (jnp.zeros((D, 4 * D), jnp.float32), jnp.zeros((D, D), jnp.float32))
    totals, x_grads = lax.scan(step, start, (inputs, cotans, segment))
    x_grad = x_grads.reshape(groups * TOK_DEV, D)
    row_grad = jax.ops.segment_sum(x_grad, item_ids, num_segments=ROWS)
    new_accum = accum + lax.optimization_barrier(jnp.sum(row_grad * row_grad, axis=1)) / D
    new_table = table - 0.5 * row_grad * lax.rsqrt(new_accum)[:, None]
    return (totals[0], totals[1], new_table, new_accum)
```

```python
import jax
import jax.numpy as jnp
from jax import lax
from jax.sharding import Mesh
from jax.sharding import PartitionSpec as P

HEAD_DIM = 64
HIGH = lax.Precision.HIGH
MP = ("y", "c")
DP = ("x", "z")


def dot(left, right, dims):
    return lax.dot_general(
        left, right, ((dims[:1], dims[1:]), ((), ())),
        precision=HIGH, preferred_element_type=jnp.float32,
    )


def body(layer_input, grad_out, segment, item_ids, w_uvqk, w_out, table, accum):
    count, width = layer_input.shape
    hd = HEAD_DIM
    scale = hd ** (-0.5)
    n_x, n_z = lax.axis_size("x"), lax.axis_size("z")
    n_mp = lax.axis_size(MP)
    pre = dot(layer_input, w_uvqk, (1, 0))
    psig = jax.nn.sigmoid(pre)
    act = pre * psig
    ublk, vblk, qblk, kblk = (act[:, i * hd:(i + 1) * hd] for i in range(4))
    seg_row = segment[0]
    place = jnp.arange(count)
    mask = ((seg_row[:, None] == seg_row[None, :]) & (place[:, None] >= place[None, :])).astype(jnp.float32)
    score = dot(qblk, kblk, (1, 1)) * scale
    sigm = jax.nn.sigmoid(score)
    attn = score * sigm * mask
    outv = dot(attn, vblk, (1, 0))
    dzval = dot(grad_out, w_out, (1, 1))
    dnorm = dzval * ublk
    stats = jnp.stack([
        jnp.sum(outv, axis=1), jnp.sum(outv * outv, axis=1),
        jnp.sum(dnorm, axis=1), jnp.sum(dnorm * outv, axis=1),
    ]).reshape(8, count // 2)
    stats = jnp.broadcast_to(stats[None], (n_mp,) + stats.shape)
    stats = jnp.sum(lax.all_to_all(stats, MP, 0, 0, tiled=True), axis=0).reshape(4, count)
    mean = stats[0] / width
    var = stats[1] / width - mean * mean
    rstd = lax.rsqrt(var + 1e-05)
    first = stats[2] / width
    second = rstd * (stats[3] - mean * stats[2]) / width
    mean, rstd, first, second = (t[:, None] for t in (mean, rstd, first, second))
    normed = (outv - mean) * rstd
    zval = normed * ublk
    dublk = dzval * normed
    dout = rstd * (dnorm - first - normed * second)
    dattn = dot(dout, vblk, (1, 1))
    dvblk = dot(attn, dout, (0, 0))
    dscore = dattn * mask * (sigm * (1.0 + score * (1.0 - sigm))) * scale
    dqblk = dot(dscore, kblk, (1, 0))
    dkblk = dot(dscore, qblk, (0, 0))
    dact = jnp.concatenate([dublk, dvblk, dqblk, dkblk], axis=1)
    dpre = dact * psig * (1.0 + pre * (1.0 - psig))
    head_part = dot(w_uvqk, dpre, (1, 1)).reshape(n_mp, width // n_mp, count)
    head_part = lax.all_to_all(head_part, MP, 0, 0, tiled=True)
    fblk = width // n_mp
    own = lax.dynamic_slice(grad_out, (0, lax.axis_index(MP) * fblk), (count, fblk))
    xgrad = jnp.sum(head_part, axis=0).T + own
    rows = n_x * n_z * n_mp
    half = n_mp // 2
    ids = jnp.arange(rows // 2, dtype=jnp.int32)
    target = (ids // half) * n_mp + ids % half
    slab = jnp.concatenate([
        dot((t[:, None] == item_ids[None, :]).astype(jnp.float32), xgrad, (1, 0))
        for t in (target, target + half)
    ], axis=1).reshape(n_x, n_z, half, 2 * fblk)
    w1 = dot(layer_input, dpre, (0, 0))
    w2 = dot(zval, grad_out, (0, 0))
    w1c = w1.reshape(n_x, n_z, 8, 2, 128).transpose(0, 1, 3, 2, 4).reshape(n_x, n_z, 16, 128)
    w2c = w2.reshape(n_z, 4, n_x, 128).transpose(2, 0, 1, 3)
    buf = jnp.concatenate([w1c, w2c, slab], axis=2).reshape(n_x, n_z * 24, 128)
    buf = jnp.sum(lax.all_to_all(buf, "x", 0, 0, tiled=True), axis=0).reshape(n_z, 24, 128)
    buf = jnp.sum(lax.all_to_all(buf, "z", 0, 0, tiled=True), axis=0)
    mine = buf[20:].reshape(half, 2, fblk).transpose(1, 0, 2).reshape(n_mp, fblk)
    row_grad = lax.all_to_all(mine, MP, 0, 0, tiled=True).reshape(1, width)
    new_accum = accum + jnp.sum(row_grad * row_grad, axis=1) / width
    new_table = table - 0.5 * row_grad * lax.rsqrt(new_accum)[:, None]
    full = jnp.broadcast_to(buf[None], (n_z, 24, 128))
    full = lax.all_to_all(full, "z", 0, 0, tiled=True)
    full = lax.all_gather(full, "x", tiled=False)
    w1g = full[:, :, :16].reshape(n_x, n_z, 2, 8, 128).transpose(0, 1, 3, 2, 4).reshape(width, 4 * hd)
    w2g = full[:, :, 16:20].transpose(1, 2, 0, 3).reshape(hd, width)
    return (w1g, w2g, new_table, new_accum)


def solution(mesh):
    split = Mesh(mesh.devices.reshape(4, 16, 4, 2), ("x", "z", "y", "c"))
    placed = (
        P(DP, None),
        P(DP, None),
        P(DP, None),
        P(DP),
        P(None, MP),
        P(MP, None),
        P(DP + MP, None),
        P(DP + MP),
    )
    return jax.shard_map(
        body,
        mesh=split,
        in_specs=placed,
        out_specs=(P(None, MP), P(MP, None), P(DP + MP, None), P(DP + MP)),
        check_vma=False,
    )
```

```python
import jax
import jax.numpy as jnp
from jax import lax
from jax.sharding import Mesh
from jax.sharding import PartitionSpec as P

HEAD_DIM = 64
HIGH = lax.Precision.HIGH
MP = ("y", "c")
DP = ("x", "z")


def dot(left, right, dims):
    return lax.dot_general(
        left, right, ((dims[:1], dims[1:]), ((), ())),
        precision=HIGH, preferred_element_type=jnp.float32,
    )


def body(layer_input, grad_out, segment, item_ids, w_uvqk, w_out, table, accum):
    count, width = layer_input.shape
    hd = HEAD_DIM
    scale = hd ** (-0.5)
    n_x, n_z = lax.axis_size("x"), lax.axis_size("z")
    n_mp = lax.axis_size(MP)
    pre = dot(layer_input, w_uvqk, (1, 0))
    psig = jax.nn.sigmoid(pre)
    act = pre * psig
    ublk, vblk, qblk, kblk = (act[:, i * hd:(i + 1) * hd] for i in range(4))
    seg_row = segment[0]
    place = jnp.arange(count)
    mask = ((seg_row[:, None] == seg_row[None, :]) & (place[:, None] >= place[None, :])).astype(jnp.float32)
    score = dot(qblk, kblk, (1, 1)) * scale
    sigm = jax.nn.sigmoid(score)
    attn = score * sigm * mask
    outv = dot(attn, vblk, (1, 0))
    dzval = dot(grad_out, w_out, (1, 1))
    dnorm = dzval * ublk
    stats = jnp.stack([
        jnp.sum(outv, axis=1), jnp.sum(outv * outv, axis=1),
        jnp.sum(dnorm, axis=1), jnp.sum(dnorm * outv, axis=1),
    ]).reshape(8, count // 2)
    stats = jnp.broadcast_to(stats[None], (n_mp,) + stats.shape)
    stats = jnp.sum(lax.all_to_all(stats, MP, 0, 0, tiled=True), axis=0).reshape(4, count)
    mean = stats[0] / width
    var = stats[1] / width - mean * mean
    rstd = lax.rsqrt(var + 1e-05)
    first = stats[2] / width
    second = rstd * (stats[3] - mean * stats[2]) / width
    mean, rstd, first, second = (t[:, None] for t in (mean, rstd, first, second))
    normed = (outv - mean) * rstd
    zval = normed * ublk
    dublk = dzval * normed
    dout = rstd * (dnorm - first - normed * second)
    dattn = dot(dout, vblk, (1, 1))
    dvblk = dot(attn, dout, (0, 0))
    dscore = dattn * mask * (sigm * (1.0 + score * (1.0 - sigm))) * scale
    dqblk = dot(dscore, kblk, (1, 0))
    dkblk = dot(dscore, qblk, (0, 0))
    dact = jnp.concatenate([dublk, dvblk, dqblk, dkblk], axis=1)
    dpre = dact * psig * (1.0 + pre * (1.0 - psig))
    head_part = dot(w_uvqk, dpre, (1, 1)).reshape(n_mp, width // n_mp, count)
    head_part = lax.all_to_all(head_part, MP, 0, 0, tiled=True)
    fblk = width // n_mp
    own = lax.dynamic_slice(grad_out, (0, lax.axis_index(MP) * fblk), (count, fblk))
    xgrad = jnp.sum(head_part, axis=0).T + own
    rows = n_x * n_z * n_mp
    half = n_mp // 2
    ids = jnp.arange(rows // 2, dtype=jnp.int32)
    target = (ids // half) * n_mp + ids % half
    slab = jnp.concatenate([
        dot((t[:, None] == item_ids[None, :]).astype(jnp.float32), xgrad, (1, 0))
        for t in (target, target + half)
    ], axis=1).reshape(n_x, n_z, half, 2 * fblk)
    w1 = dot(layer_input, dpre, (0, 0))
    w2 = dot(zval, grad_out, (0, 0))
    w1c = w1.reshape(n_x, n_z, 8, 2, 128).transpose(0, 1, 3, 2, 4).reshape(n_x, n_z, 16, 128)
    w2c = w2.reshape(n_z, 4, n_x, 128).transpose(2, 0, 1, 3)
    buf = jnp.concatenate([w1c, w2c, slab], axis=2).reshape(n_x, n_z * 24, 128)
    buf = jnp.sum(lax.all_to_all(buf, "x", 0, 0, tiled=True), axis=0).reshape(n_z, 24, 128)
    buf = jnp.sum(lax.all_to_all(buf, "z", 0, 0, tiled=True), axis=0)
    mine = lax.all_gather(buf[20:], MP, tiled=False)
    mine = mine.reshape(n_mp, half, 2, fblk)
    who = lax.axis_index(MP)
    row_grad = lax.dynamic_slice(mine, (0, who % half, who // half, 0), (n_mp, 1, 1, fblk)).reshape(1, width)
    new_accum = accum + jnp.sum(row_grad * row_grad, axis=1) / width
    new_table = table - 0.5 * row_grad * lax.rsqrt(new_accum)[:, None]
    full = jnp.broadcast_to(buf[None], (n_z, 24, 128))
    full = lax.all_to_all(full, "z", 0, 0, tiled=True)
    full = lax.all_gather(full, "x", tiled=False)
    w1g = full[:, :, :16].reshape(n_x, n_z, 2, 8, 128).transpose(0, 1, 3, 2, 4).reshape(width, 4 * hd)
    w2g = full[:, :, 16:20].transpose(1, 2, 0, 3).reshape(hd, width)
    return (w1g, w2g, new_table, new_accum)


def solution(mesh):
    split = Mesh(mesh.devices.reshape(4, 16, 4, 2), ("x", "z", "y", "c"))
    placed = (
        P(DP, None),
        P(DP, None),
        P(DP, None),
        P(DP),
        P(None, MP),
        P(MP, None),
        P(DP + MP, None),
        P(DP + MP),
    )
    return jax.shard_map(
        body,
        mesh=split,
        in_specs=placed,
        out_specs=(P(None, MP), P(MP, None), P(DP + MP, None), P(DP + MP)),
        check_vma=False,
    )
```

```python
import jax
import jax.numpy as jnp
from jax import lax
from jax.sharding import Mesh
from jax.sharding import PartitionSpec as P

HEAD_DIM = 64
HIGH = lax.Precision.HIGH
MP = ("y", "c")
DP = ("x", "h", "l")
XL = ("x", "l")


def dot(left, right, dims):
    return lax.dot_general(
        left, right, ((dims[:1], dims[1:]), ((), ())),
        precision=HIGH, preferred_element_type=jnp.float32,
    )


def body(layer_input, grad_out, segment, item_ids, w_uvqk, w_out, table, accum):
    count, width = layer_input.shape
    hd = HEAD_DIM
    scale = hd ** (-0.5)
    n_x, n_h, n_l = lax.axis_size("x"), lax.axis_size("h"), lax.axis_size("l")
    n_xl = n_x * n_l
    n_mp = lax.axis_size(MP)
    pre = dot(layer_input, w_uvqk, (1, 0))
    psig = jax.nn.sigmoid(pre)
    act = pre * psig
    ublk, vblk, qblk, kblk = (act[:, i * hd:(i + 1) * hd] for i in range(4))
    seg_row = segment[0]
    place = jnp.arange(count)
    mask = ((seg_row[:, None] == seg_row[None, :]) & (place[:, None] >= place[None, :])).astype(jnp.float32)
    score = dot(qblk, kblk, (1, 1)) * scale
    sigm = jax.nn.sigmoid(score)
    attn = score * sigm * mask
    outv = dot(attn, vblk, (1, 0))
    dzval = dot(grad_out, w_out, (1, 1))
    dnorm = dzval * ublk
    stats = jnp.stack([
        jnp.sum(outv, axis=1), jnp.sum(outv * outv, axis=1),
        jnp.sum(dnorm, axis=1), jnp.sum(dnorm * outv, axis=1),
    ]).reshape(8, count // 2)
    stats = jnp.broadcast_to(stats[None], (n_mp,) + stats.shape)
    stats = jnp.sum(lax.all_to_all(stats, MP, 0, 0, tiled=True), axis=0).reshape(4, count)
    mean = stats[0] / width
    var = stats[1] / width - mean * mean
    rstd = lax.rsqrt(var + 1e-05)
    first = stats[2] / width
    second = rstd * (stats[3] - mean * stats[2]) / width
    mean, rstd, first, second = (t[:, None] for t in (mean, rstd, first, second))
    normed = (outv - mean) * rstd
    zval = normed * ublk
    dublk = dzval * normed
    dout = rstd * (dnorm - first - normed * second)
    dattn = dot(dout, vblk, (1, 1))
    dvblk = dot(attn, dout, (0, 0))
    dscore = dattn * mask * (sigm * (1.0 + score * (1.0 - sigm))) * scale
    dqblk = dot(dscore, kblk, (1, 0))
    dkblk = dot(dscore, qblk, (0, 0))
    dact = jnp.concatenate([dublk, dvblk, dqblk, dkblk], axis=1)
    dpre = dact * psig * (1.0 + pre * (1.0 - psig))
    head_part = dot(w_uvqk, dpre, (1, 1)).reshape(n_mp, width // n_mp, count)
    head_part = lax.all_to_all(head_part, MP, 0, 0, tiled=True)
    fblk = width // n_mp
    own = lax.dynamic_slice(grad_out, (0, lax.axis_index(MP) * fblk), (count, fblk))
    xgrad = jnp.sum(head_part, axis=0).T + own
    half = n_mp // 2
    ids = jnp.arange(n_xl * n_h * half, dtype=jnp.int32)
    piece = ids // (n_h * half)
    owner = (piece // n_l) * (n_h * n_l) + (ids // half % n_h) * n_l + piece % n_l
    target = owner * n_mp + ids % half
    slab = jnp.concatenate([
        dot((t[:, None] == item_ids[None, :]).astype(jnp.float32), xgrad, (1, 0))
        for t in (target, target + half)
    ], axis=1).reshape(n_xl, n_h * half, 2 * fblk)
    w1 = dot(layer_input, dpre, (0, 0))
    w2 = dot(zval, grad_out, (0, 0))
    w1c = w1.reshape(n_xl, 4, 8, 2, 128).transpose(0, 1, 3, 2, 4).reshape(n_xl, 64, 128)
    w2c = w2.reshape(n_l, 16, n_x, 128).transpose(2, 0, 1, 3).reshape(n_xl, 16, 128)
    buf = jnp.concatenate([w1c, w2c, slab], axis=1)
    buf = jnp.sum(lax.all_to_all(buf, XL, 0, 0, tiled=True), axis=0)
    buf = jnp.broadcast_to(buf[None], (n_h, 96, 128))
    buf = jnp.sum(lax.all_to_all(buf, "h", 0, 0, tiled=True), axis=0)
    full = jnp.broadcast_to(buf[None, :80], (n_xl, 80, 128))
    full = lax.all_to_all(full, XL, 0, 0, tiled=True)
    w1g = full[:, :64].reshape(n_xl, 4, 2, 8, 128).transpose(0, 1, 3, 2, 4).reshape(width, 4 * hd)
    w2g = full[:, 64:].reshape(n_x, n_l, 16, 128).transpose(1, 2, 0, 3).reshape(hd, width)
    mine = lax.dynamic_slice(buf, (80 + half * lax.axis_index("h"), 0), (half, 128))
    mine = lax.all_gather(mine, MP, tiled=False)
    mine = mine.reshape(n_mp, half, 2, fblk)
    who = lax.axis_index(MP)
    row_grad = lax.dynamic_slice(mine, (0, who % half, who // half, 0), (n_mp, 1, 1, fblk)).reshape(1, width)
    new_accum = accum + jnp.sum(row_grad * row_grad, axis=1) / width
    new_table = table - 0.5 * row_grad * lax.rsqrt(new_accum)[:, None]
    return (w1g, w2g, new_table, new_accum)


def solution(mesh):
    split = Mesh(mesh.devices.reshape(4, 4, 4, 4, 2), ("x", "h", "l", "y", "c"))
    placed = (
        P(DP, None),
        P(DP, None),
        P(DP, None),
        P(DP),
        P(None, MP),
        P(MP, None),
        P(DP + MP, None),
        P(DP + MP),
    )
    return jax.shard_map(
        body,
        mesh=split,
        in_specs=placed,
        out_specs=(P(None, MP), P(MP, None), P(DP + MP, None), P(DP + MP)),
        check_vma=False,
    )
```

```python
import functools

import jax
import jax.numpy as jnp
from jax import lax
from jax.experimental import pallas as pl
from jax.experimental.pallas import tpu as pltpu
from jax.sharding import Mesh
from jax.sharding import PartitionSpec as P

HEAD_DIM = 64
MP = ("y", "c")
DP = ("x", "h", "l")
XL = ("x", "l")


def mm(left, right, dims):
    return lax.dot_general(
        left, right, ((dims[:1], dims[1:]), ((), ())),
        preferred_element_type=jnp.float32,
    )


def halves(value):
    high = value.astype(jnp.bfloat16)
    return high, (value - high.astype(jnp.float32)).astype(jnp.bfloat16)


def dot(left, right, dims):
    lh, ll = halves(left)
    rh, rl = halves(right)
    return mm(lh, rh, dims) + (mm(lh, rl, dims) + mm(ll, rh, dims))


def forward(*refs):
    sources, outs, held, sems = refs[:5], refs[5:11], refs[11:16], refs[16]
    copies = [
        pltpu.make_async_copy(source, target, sems.at[i])
        for i, (source, target) in enumerate(zip(sources, held))
    ]
    for copy in copies:
        copy.start()
    x_ref, w_ref, g_ref, wo_ref, seg_ref = held
    act_ref, dfac_ref, attn_ref, dsf_ref, od_ref, stats_ref = outs
    count = x_ref.shape[0]
    copies[0].wait()
    copies[1].wait()
    hd = HEAD_DIM
    scale = hd ** (-0.5)
    pre = dot(x_ref[...], w_ref[...], (1, 0))
    psig = jax.nn.sigmoid(pre)
    act = pre * psig
    act_ref[...] = act
    dfac_ref[...] = psig * (1.0 + pre * (1.0 - psig))
    ublk, vblk, qblk, kblk = (act[:, i * hd:(i + 1) * hd] for i in range(4))
    copies[4].wait()
    seg = jnp.broadcast_to(seg_ref[...].astype(jnp.float32), (count, count))
    row = lax.broadcasted_iota(jnp.int32, (count, count), 0)
    col = lax.broadcasted_iota(jnp.int32, (count, count), 1)
    mask = jnp.logical_and(seg.T == seg, row >= col)
    score = dot(qblk, kblk, (1, 1)) * scale
    sigm = jax.nn.sigmoid(score)
    attn = jnp.where(mask, score * sigm, 0.0)
    attn_ref[...] = attn
    dsf_ref[...] = jnp.where(mask, sigm * (1.0 + score * (1.0 - sigm)) * scale, 0.0)
    outv = dot(attn, vblk, (1, 0))
    copies[2].wait()
    copies[3].wait()
    dzval = dot(g_ref[...], wo_ref[...], (1, 1))
    dnorm = dzval * ublk
    od_ref[...] = jnp.concatenate([outv, dzval], axis=1)
    terms = jnp.concatenate([outv, outv * outv, dnorm, dnorm * outv], axis=1)
    pick = lax.broadcasted_iota(jnp.int32, (8, 4 * hd), 0) & 3
    blk = lax.broadcasted_iota(jnp.int32, (8, 4 * hd), 1) >> 6
    ones = (pick == blk).astype(jnp.bfloat16)
    th, tl = halves(terms)
    sums = mm(ones, th, (1, 1)) + mm(ones, tl, (1, 1))
    upper = lax.broadcasted_iota(jnp.int32, (8, 128), 0) < 4
    packed = jnp.where(upper, sums[:, :128], sums[:, 128:])
    stats_ref[...] = jnp.broadcast_to(packed[None], stats_ref.shape)


def backward(width, st_ref, act_ref, dfac_ref, attn_ref, dsf_ref, od_ref, w_ref, dpre_ref, z_ref, part_ref):
    hd = HEAD_DIM
    sums = jnp.sum(st_ref[...], axis=0)
    wide = jnp.concatenate([sums, jnp.zeros((120, 128), jnp.float32)], axis=0).T

    def column(i):
        return jnp.concatenate([wide[:, i:i + 1], wide[:, i + 4:i + 5]], axis=0)

    mean = column(0) / width
    var = column(1) / width - mean * mean
    rstd = lax.rsqrt(var + 1e-05)
    first = column(2) / width
    second = rstd * (column(3) - mean * column(2)) / width
    act = act_ref[...]
    ublk, vblk, qblk, kblk = (act[:, i * hd:(i + 1) * hd] for i in range(4))
    outv, dzval = od_ref[:, :hd], od_ref[:, hd:]
    normed = (outv - mean) * rstd
    z_ref[...] = normed * ublk
    dnorm = dzval * ublk
    dout = rstd * (dnorm - first - normed * second)
    dattn = dot(dout, vblk, (1, 1))
    dvblk = dot(attn_ref[...], dout, (0, 0))
    dscore = dattn * dsf_ref[...]
    dqblk = dot(dscore, kblk, (1, 0))
    dkblk = dot(dscore, qblk, (0, 0))
    dpre = jnp.concatenate([dzval * normed, dvblk, dqblk, dkblk], axis=1) * dfac_ref[...]
    dpre_ref[...] = dpre
    part_ref[...] = dot(w_ref[...], dpre, (1, 1))


def packing(recv_ref, own_ref, ids_ref, w1_ref, w2_ref, buf_ref):
    xgrad = jnp.sum(recv_ref[...], axis=0) + own_ref[...]
    xh, xl = halves(xgrad)
    count = xgrad.shape[1]
    ids = jnp.broadcast_to(ids_ref[...], (256, count))
    spot = lax.broadcasted_iota(jnp.int32, (256, count), 0)
    piece = spot >> 4
    owner = ((piece >> 2) << 4) + (((spot >> 2) & 3) << 2) + (piece & 3)
    target = (owner << 3) + (spot & 3)
    sides = []
    for shift in (0, 4):
        hits = (ids == target + shift).astype(jnp.float32).astype(jnp.bfloat16)
        sides.append(mm(hits, xh, (1, 1)) + mm(hits, xl, (1, 1)))
    slab = jnp.concatenate(sides, axis=1)
    for n in range(16):
        for t in range(4):
            for a in range(2):
                buf_ref[n, t * 16 + a * 8:t * 16 + a * 8 + 8, :] = w1_ref[
                    n * 32 + t * 8:n * 32 + t * 8 + 8, a * 128:a * 128 + 128]
        x, l = n // 4, n % 4
        buf_ref[n, 64:80, :] = w2_ref[l * 16:l * 16 + 16, x * 128:x * 128 + 128]
        buf_ref[n, 80:96, :] = slab[n * 16:n * 16 + 16]


def call(kernel, *shapes, plain=(), loose=(), remote=None):
    extra = {}
    if remote:
        extra = dict(
            in_specs=[pl.BlockSpec(memory_space=pltpu.HBM) for _ in remote],
            scratch_shapes=[pltpu.VMEM(t.shape, t.dtype) for t in remote]
            + [pltpu.SemaphoreType.DMA((len(remote),))],
        )
    run = pl.pallas_call(
        kernel,
        out_shape=[
            jax.ShapeDtypeStruct(t, jnp.float32) if i in plain else pltpu.VMEM(t, jnp.float32)
            for i, t in enumerate(shapes)
        ],
        compiler_params=pltpu.CompilerParams(vmem_limit_bytes=16 << 20),
        **extra,
    )

    def with_vmem(*args):
        return run(*(
            pltpu.with_memory_space_constraint(t, pltpu.HBM if i in loose else pltpu.VMEM)
            for i, t in enumerate(args)
        ))
    return with_vmem


def body(layer_input, grad_out, segment, item_ids, w_uvqk, w_out, table, accum):
    count, width = layer_input.shape
    hd = HEAD_DIM
    n_x, n_h, n_l = lax.axis_size("x"), lax.axis_size("h"), lax.axis_size("l")
    n_xl = n_x * n_l
    n_mp = lax.axis_size(MP)
    fblk = width // n_mp
    half = n_mp // 2
    square = (count, count)
    given = (layer_input, w_uvqk, grad_out, w_out, segment)
    act, dfac, attn, dsf, od, stats = call(
        forward, (count, 4 * hd), (count, 4 * hd), square, square, (count, 2 * hd), (n_mp, 8, 128),
        plain=(5,), loose=(0, 1, 2, 3, 4), remote=given,
    )(*given)
    own = lax.dynamic_slice(grad_out, (0, lax.axis_index(MP) * fblk), (count, fblk)).T
    stats = lax.all_to_all(stats, MP, 0, 0, tiled=True)
    dpre, zval, part = call(
        functools.partial(backward, width), (count, 4 * hd), (count, hd), (width, count), plain=(2,),
    )(stats, act, dfac, attn, dsf, od, w_uvqk)
    part = lax.all_to_all(part.reshape(n_mp, fblk, count), MP, 0, 0, tiled=True)
    w1 = lax.dot_general(
        layer_input, dpre, (((0,), (0,)), ((), ())),
        precision=lax.Precision.HIGH, preferred_element_type=jnp.float32)
    w2 = lax.dot_general(
        zval, grad_out, (((0,), (0,)), ((), ())),
        precision=lax.Precision.HIGH, preferred_element_type=jnp.float32)
    buf, = call(packing, (n_xl, 96, 128))(part, own, item_ids.reshape(1, count), w1, w2)
    buf = jnp.sum(lax.all_to_all(buf, XL, 0, 0, tiled=True), axis=0)
    buf = jnp.broadcast_to(buf[None], (n_h, 96, 128))
    buf = jnp.sum(lax.all_to_all(buf, "h", 0, 0, tiled=True), axis=0)
    full = jnp.broadcast_to(buf[None, :80], (n_xl, 80, 128))
    full = lax.all_to_all(full, XL, 0, 0, tiled=True)
    w1g = full[:, :64].reshape(n_xl, 4, 2, 8, 128).transpose(0, 1, 3, 2, 4).reshape(width, 4 * hd)
    w2g = full[:, 64:].reshape(n_x, n_l, 16, 128).transpose(1, 2, 0, 3).reshape(hd, width)
    mine = lax.dynamic_slice(buf, (80 + half * lax.axis_index("h"), 0), (half, 128))
    mine = lax.all_gather(lax.all_gather(mine, "c", tiled=False), "y", tiled=False)
    mine = mine.reshape(n_mp, half, 2, fblk)
    who = lax.axis_index(MP)
    row_grad = lax.dynamic_slice(mine, (0, who % half, who // half, 0), (n_mp, 1, 1, fblk)).reshape(1, width)
    new_accum = accum + jnp.sum(row_grad * row_grad, axis=1) / width
    new_table = table - 0.5 * row_grad * lax.rsqrt(new_accum)[:, None]
    return (w1g, w2g, new_table, new_accum)


def solution(mesh):
    split = Mesh(mesh.devices.reshape(4, 4, 4, 4, 2), ("x", "h", "l", "y", "c"))
    placed = (
        P(DP, None),
        P(DP, None),
        P(DP, None),
        P(DP),
        P(None, MP),
        P(MP, None),
        P(DP + MP, None),
        P(DP + MP),
    )
    return jax.shard_map(
        body,
        mesh=split,
        in_specs=placed,
        out_specs=(P(None, MP), P(MP, None), P(DP + MP, None), P(DP + MP)),
        check_vma=False,
    )
```

```python
import functools

import jax
import jax.numpy as jnp
from jax import lax
from jax.experimental import pallas as pl
from jax.experimental.pallas import tpu as pltpu
from jax.sharding import Mesh
from jax.sharding import PartitionSpec as P

HEAD_DIM = 64
MP = ("y", "c")
DP = ("x", "h", "l")
XL = ("x", "l")


def mm(left, right, dims):
    return lax.dot_general(
        left, right, ((dims[:1], dims[1:]), ((), ())),
        preferred_element_type=jnp.float32,
    )


def halves(value):
    high = value.astype(jnp.bfloat16)
    return high, (value - high.astype(jnp.float32)).astype(jnp.bfloat16)


def dot(left, right, dims):
    lh, ll = halves(left)
    rh, rl = halves(right)
    return mm(lh, rh, dims) + (mm(lh, rl, dims) + mm(ll, rh, dims))


def forward(*refs):
    sources, outs, held, sems = refs[:5], refs[5:11], refs[11:16], refs[16]
    copies = [
        pltpu.make_async_copy(source, target, sems.at[i])
        for i, (source, target) in enumerate(zip(sources, held))
    ]
    for copy in copies:
        copy.start()
    x_ref, w_ref, g_ref, wo_ref, seg_ref = held
    act_ref, dfac_ref, attn_ref, dsf_ref, od_ref, stats_ref = outs
    count = x_ref.shape[0]
    copies[0].wait()
    copies[1].wait()
    hd = HEAD_DIM
    scale = hd ** (-0.5)
    pre = dot(x_ref[...], w_ref[...], (1, 0))
    psig = jax.nn.sigmoid(pre)
    act = pre * psig
    act_ref[...] = act
    dfac_ref[...] = psig * (1.0 + pre * (1.0 - psig))
    ublk, vblk, qblk, kblk = (act[:, i * hd:(i + 1) * hd] for i in range(4))
    copies[4].wait()
    seg = jnp.broadcast_to(seg_ref[...].astype(jnp.float32), (count, count))
    row = lax.broadcasted_iota(jnp.int32, (count, count), 0)
    col = lax.broadcasted_iota(jnp.int32, (count, count), 1)
    mask = jnp.logical_and(seg.T == seg, row >= col)
    score = dot(qblk, kblk, (1, 1)) * scale
    sigm = jax.nn.sigmoid(score)
    attn = jnp.where(mask, score * sigm, 0.0)
    attn_ref[...] = attn
    dsf_ref[...] = jnp.where(mask, sigm * (1.0 + score * (1.0 - sigm)) * scale, 0.0)
    outv = dot(attn, vblk, (1, 0))
    copies[2].wait()
    copies[3].wait()
    dzval = dot(g_ref[...], wo_ref[...], (1, 1))
    dnorm = dzval * ublk
    od_ref[...] = jnp.concatenate([outv, dzval], axis=1)
    terms = jnp.concatenate([outv, outv * outv, dnorm, dnorm * outv], axis=1)
    pick = lax.broadcasted_iota(jnp.int32, (8, 4 * hd), 0) & 3
    blk = lax.broadcasted_iota(jnp.int32, (8, 4 * hd), 1) >> 6
    ones = (pick == blk).astype(jnp.bfloat16)
    th, tl = halves(terms)
    sums = mm(ones, th, (1, 1)) + mm(ones, tl, (1, 1))
    upper = lax.broadcasted_iota(jnp.int32, (8, 128), 0) < 4
    packed = jnp.where(upper, sums[:, :128], sums[:, 128:])
    stats_ref[...] = jnp.broadcast_to(packed[None], stats_ref.shape)


def backward(width, st_ref, act_ref, dfac_ref, attn_ref, dsf_ref, od_ref, w_ref, dpre_ref, z_ref, part_ref):
    hd = HEAD_DIM
    sums = jnp.sum(st_ref[...], axis=0)
    wide = jnp.concatenate([sums, jnp.zeros((120, 128), jnp.float32)], axis=0).T

    def column(i):
        return jnp.concatenate([wide[:, i:i + 1], wide[:, i + 4:i + 5]], axis=0)

    mean = column(0) / width
    var = column(1) / width - mean * mean
    rstd = lax.rsqrt(var + 1e-05)
    first = column(2) / width
    second = rstd * (column(3) - mean * column(2)) / width
    act = act_ref[...]
    ublk, vblk, qblk, kblk = (act[:, i * hd:(i + 1) * hd] for i in range(4))
    outv, dzval = od_ref[:, :hd], od_ref[:, hd:]
    normed = (outv - mean) * rstd
    z_ref[...] = normed * ublk
    dnorm = dzval * ublk
    dout = rstd * (dnorm - first - normed * second)
    dattn = dot(dout, vblk, (1, 1))
    dvblk = dot(attn_ref[...], dout, (0, 0))
    dscore = dattn * dsf_ref[...]
    dqblk = dot(dscore, kblk, (1, 0))
    dkblk = dot(dscore, qblk, (0, 0))
    dpre = jnp.concatenate([dzval * normed, dvblk, dqblk, dkblk], axis=1) * dfac_ref[...]
    dpre_ref[...] = dpre
    part_ref[...] = dot(w_ref[...], dpre, (1, 1))


def packing(recv_ref, own_ref, ids_ref, w1_ref, w2_ref, buf_ref):
    xgrad = jnp.sum(recv_ref[...], axis=0) + own_ref[...]
    xh, xl = halves(xgrad)
    count = xgrad.shape[1]
    ids = jnp.broadcast_to(ids_ref[...], (256, count))
    spot = lax.broadcasted_iota(jnp.int32, (256, count), 0)
    piece = spot >> 4
    owner = ((piece >> 2) << 4) + (((spot >> 2) & 3) << 2) + (piece & 3)
    target = (owner << 3) + (spot & 3)
    sides = []
    for shift in (0, 4):
        hits = (ids == target + shift).astype(jnp.float32).astype(jnp.bfloat16)
        sides.append(mm(hits, xh, (1, 1)) + mm(hits, xl, (1, 1)))
    slab = jnp.concatenate(sides, axis=1)
    for n in range(16):
        for t in range(4):
            for a in range(2):
                buf_ref[n, t * 16 + a * 8:t * 16 + a * 8 + 8, :] = w1_ref[
                    n * 32 + t * 8:n * 32 + t * 8 + 8, a * 128:a * 128 + 128]
        x, l = n // 4, n % 4
        buf_ref[n, 64:80, :] = w2_ref[l * 16:l * 16 + 16, x * 128:x * 128 + 128]
        buf_ref[n, 80:96, :] = slab[n * 16:n * 16 + 16]


def call(kernel, *shapes, plain=(), loose=(), remote=None):
    extra = {}
    if remote:
        extra = dict(
            in_specs=[pl.BlockSpec(memory_space=pltpu.HBM) for _ in remote],
            scratch_shapes=[pltpu.VMEM(t.shape, t.dtype) for t in remote]
            + [pltpu.SemaphoreType.DMA((len(remote),))],
        )
    run = pl.pallas_call(
        kernel,
        out_shape=[
            jax.ShapeDtypeStruct(t, jnp.float32) if i in plain else pltpu.VMEM(t, jnp.float32)
            for i, t in enumerate(shapes)
        ],
        compiler_params=pltpu.CompilerParams(vmem_limit_bytes=16 << 20),
        **extra,
    )

    def with_vmem(*args):
        return run(*(
            pltpu.with_memory_space_constraint(t, pltpu.HBM if i in loose else pltpu.VMEM)
            for i, t in enumerate(args)
        ))
    return with_vmem


def body(layer_input, grad_out, segment, item_ids, w_uvqk, w_out, table, accum):
    count, width = layer_input.shape
    hd = HEAD_DIM
    n_x, n_h, n_l = lax.axis_size("x"), lax.axis_size("h"), lax.axis_size("l")
    n_xl = n_x * n_l
    n_mp = lax.axis_size(MP)
    fblk = width // n_mp
    half = n_mp // 2
    square = (count, count)
    given = (layer_input, w_uvqk, grad_out, w_out, segment)
    act, dfac, attn, dsf, od, stats = call(
        forward, (count, 4 * hd), (count, 4 * hd), square, square, (count, 2 * hd), (n_mp, 8, 128),
        plain=(5,), loose=(0, 1, 2, 3, 4), remote=given,
    )(*given)
    own = lax.dynamic_slice(grad_out, (0, lax.axis_index(MP) * fblk), (count, fblk)).T
    stats = lax.all_to_all(stats, MP, 0, 0, tiled=True)
    dpre, zval, part = call(
        functools.partial(backward, width), (count, 4 * hd), (count, hd), (width, count), plain=(2,),
    )(stats, act, dfac, attn, dsf, od, w_uvqk)
    part = lax.all_to_all(part.reshape(n_mp, fblk, count), MP, 0, 0, tiled=True)
    w1 = lax.dot_general(
        layer_input, dpre, (((0,), (0,)), ((), ())),
        precision=lax.Precision.HIGH, preferred_element_type=jnp.float32)
    w2 = lax.dot_general(
        zval, grad_out, (((0,), (0,)), ((), ())),
        precision=lax.Precision.HIGH, preferred_element_type=jnp.float32)
    buf, = call(packing, (n_xl, 96, 128))(part, own, item_ids.reshape(1, count), w1, w2)
    buf = jnp.sum(lax.all_to_all(buf, XL, 0, 0, tiled=True), axis=0)
    buf = jnp.broadcast_to(buf[None], (n_h, 96, 128))
    buf = jnp.sum(lax.all_to_all(buf, "h", 0, 0, tiled=True), axis=0)
    full = jnp.broadcast_to(buf[None, :80], (n_xl, 80, 128))
    full = lax.all_to_all(full, XL, 0, 0, tiled=True)
    w1g = full[:, :64].reshape(n_xl, 4, 2, 8, 128).transpose(0, 1, 3, 2, 4).reshape(width, 4 * hd)
    w2g = full[:, 64:].reshape(n_x, n_l, 16, 128).transpose(1, 2, 0, 3).reshape(hd, width)
    mine = lax.dynamic_slice(buf, (80 + half * lax.axis_index("h"), 0), (half, 128))
    mine = lax.all_gather(mine, MP, tiled=False)
    mine = mine.reshape(n_mp, half, 2, fblk)
    who = lax.axis_index(MP)
    row_grad = lax.dynamic_slice(mine, (0, who % half, who // half, 0), (n_mp, 1, 1, fblk)).reshape(1, width)
    new_accum = accum + jnp.sum(row_grad * row_grad, axis=1) / width
    new_table = table - 0.5 * row_grad * lax.rsqrt(new_accum)[:, None]
    return (w1g, w2g, new_table, new_accum)


def solution(mesh):
    split = Mesh(mesh.devices.reshape(4, 4, 4, 4, 2), ("x", "h", "l", "y", "c"))
    placed = (
        P(DP, None),
        P(DP, None),
        P(DP, None),
        P(DP),
        P(None, MP),
        P(MP, None),
        P(DP + MP, None),
        P(DP + MP),
    )
    return jax.shard_map(
        body,
        mesh=split,
        in_specs=placed,
        out_specs=(P(None, MP), P(MP, None), P(DP + MP, None), P(DP + MP)),
        check_vma=False,
    )
```
